32 devices in a mesh: stn: 4 (over y, x), chan: 4 (over z), beam: 2 (over core).
Axes of the slice: x: 2, y: 2, z: 4, core: 2. Of those that a mesh axis runs over, the one named last changes fastest.
Arguments:
- volts: bfloat16 [2, 128, 12, 9216], P(None, 'stn', 'chan', 'beam'), may hold values from -6 to 6
- taps: float32 [16, 256], replicated, may hold values from -1.5 to 1.5
- delays: int32 [32, 128], P(None, 'stn'), may hold values from 0 to 1023
- station_sub: int32 [128], P('stn'), may hold values from 0 to 3
- beam_sub: int32 [32], replicated, may hold values from 0 to 3
Outputs:
- beams: float32 [32, 2, 12, 48, 256], P(('stn', 'chan', 'beam'))
The draws below stay inside these ranges and needn't reach their ends.
All inputs are finite; a program needn't handle non-finite values.
Results may differ from the reference program's by a relative error of at most 0.014.
Values may be sent and summed in bfloat16 or wider, within the bound.
A program may use at most 192 MiB of HBM per device.

```python
import math
import jax
import jax.numpy as jnp
from jax import lax

FINE = 256
TAPS = 16
STN_DEV = 32
SUBARRAYS = 4
STATIONS = 128
CHANNELS = 12
FRAMES = 48
SAMPLES = 9216
BEAMS = 32
N_STN = 4


def set_ends(drawn, key, low, top_value):
    dims = drawn.shape
    spot = [jax.random.randint(jax.random.fold_in(key, axis), (), 0, dims[axis]) for axis in range(len(dims))]
    drawn = drawn.at[tuple(spot)].set(low)
    longest = dims.index(max(dims))
    spot[longest] = (spot[longest] + 1) % dims[longest]
    return drawn.at[tuple(spot)].set(top_value)


def steps_of(own_key, extent, shards, low, high):
    loudness, own = 1.0, jax.random.fold_in(own_key, 6)
    for position, blocks in shards:
        steps = jnp.exp(jax.random.uniform(jax.random.fold_in(own, position), (blocks,), jnp.float32, low / len(shards), high / len(shards)))
        loudness = loudness * jnp.repeat(steps, extent[position] // blocks).reshape([-1 if axis == position else 1 for axis in range(len(extent))])
    return loudness


def noise(rng, shape, scale, limit, cuts=(), kind=jnp.bfloat16):
    factor_of = steps_of(rng, shape, cuts, -0.22, 0.18) if cuts else 1.0
    values = jax.random.normal(rng, shape, jnp.float32) * scale * factor_of
    return jnp.minimum(jnp.maximum(values, -limit), limit).astype(kind)


def setup_inputs(seed: int = 0) -> dict:
    arg_keys = jax.random.split(jax.random.key(seed), 6)
    return {
        "volts": noise(arg_keys[0], (2, STATIONS, CHANNELS, SAMPLES), 1.0, 6.0, ((1, 4), (2, 4), (3, 2))),
        "taps": noise(arg_keys[1], (TAPS, FINE), 0.25, 1.5, (), jnp.float32),
        "delays": set_ends(jax.random.randint(arg_keys[2], (BEAMS, STATIONS), 0, 1024), jax.random.fold_in(arg_keys[2], 1), 0, 1023).astype(jnp.int32),
        "station_sub": set_ends(jax.random.randint(arg_keys[3], (STATIONS,), 0, SUBARRAYS), jax.random.fold_in(arg_keys[3], 1), 0, SUBARRAYS - 1).astype(jnp.int32),
        "beam_sub": set_ends(jax.random.randint(arg_keys[4], (BEAMS,), 0, SUBARRAYS), jax.random.fold_in(arg_keys[4], 1), 0, SUBARRAYS - 1).astype(jnp.int32),
    }


def filter_frames(extended, taps, frame_count):
    tap_count, fine = taps.shape
    hop = 3 * fine // 4
    groups = frame_count // 4
    rows = groups + (tap_count + 2) // 3
    shape = extended.shape
    needed = 3 * hop + 3 * rows * fine
    padding = max(0, needed - shape[-1])
    padded = jnp.concatenate([extended, jnp.zeros(shape[:-1] + (padding,), extended.dtype)], axis=-1)
    streams = []
    for phase in range(4):
        start = phase * hop
        piece = lax.slice_in_dim(padded, start, start + 3 * rows * fine, 1, len(shape) - 1)
        streams.append(piece.reshape(shape[:-1] + (rows, 3, fine)))
    stacked = jnp.stack(streams, axis=-2)
    axis = len(shape) - 1
    total = None
    for tap in range(tap_count):
        lead = tap // 3
        inner = tap % 3
        window = lax.slice_in_dim(stacked, lead, lead + groups, 1, axis)[..., inner, :, :].astype(jnp.float32)
        term = taps[tap] * window
        total = term if total is None else total + term
    return total.reshape(shape[:-1] + (frame_count, fine)).astype(jnp.bfloat16)

def dft_tables(fine):
    index = jnp.arange(fine, dtype=jnp.int32)
    product = index[:, None] * index[None, :] % fine
    angle = 2.0 * jnp.pi * product.astype(jnp.float32) / fine
    scale = 1.0 / math.sqrt(fine)
    return ((jnp.cos(angle) * scale).astype(jnp.bfloat16), (jnp.sin(angle) * scale).astype(jnp.bfloat16))

def channelize(filtered, frame_start, hop):
    fine = filtered.shape[-1]
    cosine, sine = dft_tables(fine)
    spec_re = jnp.einsum('...j,jk->...k', filtered[0], cosine, preferred_element_type=jnp.float32) + jnp.einsum('...j,jk->...k', filtered[1], sine, preferred_element_type=jnp.float32)
    spec_im = jnp.einsum('...j,jk->...k', filtered[1], cosine, preferred_element_type=jnp.float32) - jnp.einsum('...j,jk->...k', filtered[0], sine, preferred_element_type=jnp.float32)
    frame_count = filtered.shape[-2]
    frame_index = frame_start + jnp.arange(frame_count, dtype=jnp.int32)
    fine_index = jnp.arange(fine, dtype=jnp.int32)
    turn = fine_index[None, :] * hop % fine * frame_index[:, None] % fine
    rot = 2.0 * jnp.pi * turn.astype(jnp.float32) / fine
    cos_rot = jnp.cos(rot)
    sin_rot = jnp.sin(rot)
    out_re = spec_re * cos_rot + spec_im * sin_rot
    out_im = spec_im * cos_rot - spec_re * sin_rot
    return jnp.stack([out_re, out_im]).astype(jnp.bfloat16)

def steering(delay_rows, beam_subs, station_subs, chan_start, chan_count, fine, amplitude):
    fine_index = jnp.arange(fine, dtype=jnp.int32)
    chan_index = chan_start + jnp.arange(chan_count, dtype=jnp.int32)
    freq_index = chan_index[:, None] * fine + fine_index[None, :]
    turn = delay_rows[:, :, None, None] * freq_index[None, None, :, :] % 65536
    phase = 2.0 * jnp.pi * turn.astype(jnp.float32) / 65536.0
    member = (beam_subs[:, None] == station_subs[None, :]).astype(jnp.float32)[:, :, None, None]
    weight_re = (amplitude * member * jnp.cos(phase)).astype(jnp.bfloat16)
    weight_im = (-amplitude * member * jnp.sin(phase)).astype(jnp.bfloat16)
    return (weight_re, weight_im)

def reference(volts, taps, delays, station_sub, beam_sub):
    hop = 3 * FINE // 4
    extra = TAPS * FINE - hop
    amplitude = 1.0 / math.sqrt(STATIONS // SUBARRAYS)

    def one_channel(chan):
        raw = lax.dynamic_slice_in_dim(volts, chan, 1, 2)
        extended = jnp.concatenate([raw, jnp.zeros((2, STATIONS, 1, extra), jnp.bfloat16)], axis=3)
        filtered = filter_frames(extended, taps, FRAMES)
        spectra = channelize(filtered, 0, hop)
        weight_re, weight_im = steering(delays, beam_sub, station_sub, chan, 1, FINE, amplitude)
        grouped = spectra.reshape(2, N_STN, STN_DEV, 1, FRAMES, FINE).astype(jnp.float32)
        w_re = weight_re.reshape(BEAMS, N_STN, STN_DEV, 1, FINE).astype(jnp.float32)
        w_im = weight_im.reshape(BEAMS, N_STN, STN_DEV, 1, FINE).astype(jnp.float32)
        form = 'bgsck,gscfk->gbcfk'
        part_re = jnp.einsum(form, w_re, grouped[0]) - jnp.einsum(form, w_im, grouped[1])
        part_im = jnp.einsum(form, w_re, grouped[1]) + jnp.einsum(form, w_im, grouped[0])
        part_re = part_re.astype(jnp.bfloat16).astype(jnp.float32)
        part_im = part_im.astype(jnp.bfloat16).astype(jnp.float32)
        total_re = lax.optimization_barrier(jnp.sum(part_re, axis=0))[:, 0]
        total_im = lax.optimization_barrier(jnp.sum(part_im, axis=0))[:, 0]
        return jnp.stack([total_re, total_im], axis=1)
    per_channel = lax.map(one_channel, jnp.arange(CHANNELS, dtype=jnp.int32))
    return jnp.transpose(per_channel, (1, 2, 0, 3, 4))
```

```python
import functools
import math

import jax
import jax.numpy as jnp
import numpy as np
from jax import lax
from jax.experimental import pallas as pl
from jax.experimental.pallas import tpu as pltpu
from jax.sharding import PartitionSpec as P

SUBARRAYS = 4
UNROLL = 4
LANES = 128


def dft_tables(fine):
    index = np.arange(fine)
    angle = 2.0 * np.pi * (index[:, None] * index[None, :] % fine) / fine
    scale = 1.0 / math.sqrt(fine)
    return (
        jnp.asarray(np.cos(angle) * scale, jnp.bfloat16),
        jnp.asarray(np.sin(angle) * scale, jnp.bfloat16),
    )


def unit_turn(turn):
    quarter = (turn + 8192) >> 14
    t = (turn - (quarter << 14)).astype(jnp.float32) * (2.0 * math.pi / 65536.0)
    u = t * t
    sine = t * (1.0 + u * (-1.0 / 6 + u * (1.0 / 120 + u * (-1.0 / 5040))))
    cosine = 1.0 + u * (-0.5 + u * (1.0 / 24 + u * (-1.0 / 720 + u * (1.0 / 40320))))
    odd = (quarter & 1) == 1
    c = jnp.where(odd, sine, cosine)
    s = jnp.where(odd, cosine, sine)
    c = jnp.where(((quarter + 1) & 2) == 2, -c, c)
    s = jnp.where((quarter & 2) == 2, -s, s)
    return c, s


def beam_kernel(
    amplitude,
    station_sub,
    beam_sub,
    start,
    delay_ref,
    taps_ref,
    cos_ref,
    sin_ref,
    own_ref,
    next_ref,
    out_ref,
    table,
    wide,
    half,
    filtered,
    spec,
    x_ref,
    w_ref,
    members,
    counts,
):
    tap_count, fine = taps_ref.shape
    stations = own_ref.shape[2]
    samples = own_ref.shape[3]
    beams = out_ref.shape[0]
    frames = out_ref.shape[3]
    groups = frames // 4
    parts = fine // LANES
    row = stations + UNROLL
    chan = pl.program_id(0)

    @pl.when(chan == 0)
    def _():
        for sub in range(SUBARRAYS):
            def add(s, n, sub=sub):
                members[sub * row + n] = s
                return n + jnp.where(station_sub[s] == sub, 1, 0)

            count = lax.fori_loop(0, stations, add, jnp.int32(0))
            for extra in range(UNROLL):
                members[sub * row + count + extra] = stations
            counts[sub] = (count + UNROLL - 1) // UNROLL
        for part in range(2 * parts):
            x_ref[part, stations] = jnp.zeros((frames, LANES), jnp.float32)
            w_ref[part, pl.ds(stations, 8), :] = jnp.zeros((8, LANES), jnp.float32)
        cosine = cos_ref[...].astype(jnp.float32)
        sine = sin_ref[...].astype(jnp.float32)
        k = lax.broadcasted_iota(jnp.int32, (fine, fine), 1)
        for phase in range(4):
            q = (3 * phase * k) & 3
            cq = jnp.where(q == 0, 1.0, jnp.where(q == 2, -1.0, 0.0))
            sq = jnp.where(q == 1, 1.0, jnp.where(q == 3, -1.0, 0.0))
            same = (cosine * cq - sine * sq).astype(jnp.bfloat16)
            cross = sine * cq + cosine * sq
            table[phase, 0:fine, 0:fine] = same
            table[phase, fine:, fine:] = same
            table[phase, fine:, 0:fine] = cross.astype(jnp.bfloat16)
            table[phase, 0:fine, fine:] = (-cross).astype(jnp.bfloat16)

    for ri in range(2):
        wide[ri, :, 0:samples] = own_ref[ri, 0].astype(jnp.float32)
        wide[ri, :, samples:] = next_ref[ri, 0].astype(jnp.float32)
        shift = fine // 4
        length = half.shape[2]
        half[ri] = wide[ri, :, shift : shift + length]

    hop = 3 * fine // 4

    @pl.loop(0, groups)
    def _(g):
        for phase in range(4):
            source = wide if phase % 2 == 0 else half
            base = phase * hop - (0 if phase % 2 == 0 else fine // 4)
            for ri in range(2):
                total = None
                for tap in range(tap_count):
                    at = pl.multiple_of(g * 3 * fine + (base + tap * fine), LANES)
                    term = taps_ref[tap : tap + 1, :] * source[ri, :, pl.ds(at, fine)]
                    total = term if total is None else total + term
                filtered[phase, pl.ds(pl.multiple_of(g * stations, stations), stations), ri * fine : (ri + 1) * fine] = (
                    total.astype(jnp.bfloat16)
                )

    for phase in range(4):
        result = jnp.dot(filtered[phase], table[phase], preferred_element_type=jnp.float32)
        for g in range(groups):
            at = (4 * g + phase) * stations
            for part in range(2 * parts):
                spec[part, at : at + stations, :] = result[
                    g * stations : (g + 1) * stations, part * LANES : (part + 1) * LANES
                ]
    for s in range(stations):
        for part in range(2 * parts):
            x_ref[part, s] = spec.at[part][pl.ds(s, frames, stride=stations), :]

    lane = lax.broadcasted_iota(jnp.int32, (stations, LANES), 1)
    first = (start[0] + chan) * fine

    @pl.loop(0, beams)
    def _(b):
        delay = delay_ref[b]
        for part in range(parts):
            turn = (delay * (lane + (first + part * LANES))) & 65535
            c, s = unit_turn(turn)
            w_ref[part, 0:stations, :] = c * amplitude
            w_ref[parts + part, 0:stations, :] = s * (-amplitude)
        sub = beam_sub[b]

        def add(i, carry):
            totals = list(carry)
            for u in range(UNROLL):
                s = members[sub * row + i * UNROLL + u]
                for part in range(parts):
                    w_re = w_ref.at[part][pl.ds(s, 8, stride=0), :][None]
                    w_im = w_ref.at[parts + part][pl.ds(s, 8, stride=0), :][None]
                    x_re = x_ref[part, s].reshape(frames // 8, 8, LANES)
                    x_im = x_ref[parts + part, s].reshape(frames // 8, 8, LANES)
                    totals[part] = totals[part] + (w_re * x_re - w_im * x_im)
                    totals[parts + part] = totals[parts + part] + (w_re * x_im + w_im * x_re)
            return tuple(totals)

        zero = jnp.zeros((frames // 8, 8, LANES), jnp.float32)
        totals = lax.fori_loop(0, counts[sub], add, (zero,) * (2 * parts))
        for part in range(parts):
            lanes = slice(part * LANES, (part + 1) * LANES)
            out_ref[b, 0, 0, :, lanes] = totals[part].reshape(frames, LANES).astype(jnp.bfloat16)
            out_ref[b, 1, 0, :, lanes] = totals[parts + part].reshape(frames, LANES).astype(jnp.bfloat16)


def beam_sums(own, following, taps, delays, station_sub, beam_sub, chan_start, amplitude):
    tap_count, fine = taps.shape
    chans, stations, samples = own.shape[1:]
    beams = delays.shape[0]
    hop = 3 * fine // 4
    frames = samples // hop
    parts = fine // LANES
    cosine, sine = dft_tables(fine)
    delay = jnp.broadcast_to(delays[:, :, None], (beams, stations, LANES))
    whole = lambda *shape: pl.BlockSpec(shape, lambda c, *_: (0,) * len(shape))
    volts_spec = pl.BlockSpec((2, 1, stations, samples), lambda c, *_: (0, c, 0, 0))
    length = 2 * samples - LANES
    return pl.pallas_call(
        functools.partial(beam_kernel, amplitude),
        out_shape=jax.ShapeDtypeStruct((beams, 2, chans, frames, fine), jnp.bfloat16),
        grid_spec=pltpu.PrefetchScalarGridSpec(
            num_scalar_prefetch=3,
            grid=(chans,),
            in_specs=[
                whole(beams, stations, LANES),
                whole(tap_count, fine),
                whole(fine, fine),
                whole(fine, fine),
                volts_spec,
                volts_spec,
            ],
            out_specs=pl.BlockSpec((beams, 2, 1, frames, fine), lambda c, *_: (0, 0, c, 0, 0)),
            scratch_shapes=[
                pltpu.VMEM((4, 2 * fine, 2 * fine), jnp.bfloat16),
                pltpu.VMEM((2, stations, 2 * samples), jnp.float32),
                pltpu.VMEM((2, stations, length), jnp.float32),
                pltpu.VMEM((4, frames // 4 * stations, 2 * fine), jnp.bfloat16),
                pltpu.VMEM((2 * parts, (frames + 1) * stations, LANES), jnp.float32),
                pltpu.VMEM((2 * parts, stations + 1, frames, LANES), jnp.float32),
                pltpu.VMEM((2 * parts, stations + 8, LANES), jnp.float32),
                pltpu.SMEM((SUBARRAYS * (stations + UNROLL),), jnp.int32),
                pltpu.SMEM((SUBARRAYS,), jnp.int32),
            ],
        ),
        compiler_params=pltpu.CompilerParams(dimension_semantics=("arbitrary",)),
        name="beam_sums",
    )(station_sub, beam_sub, chan_start, delay, taps, cosine, sine, own, following)


def body(volts, taps, delays, station_sub, beam_sub):
    own = jnp.transpose(volts, (0, 2, 1, 3))
    size = lax.axis_size("beam")
    following = lax.ppermute(own, "beam", [(i, i - 1) for i in range(1, size)])
    chans = own.shape[1]
    chan_start = (lax.axis_index("chan") * chans).astype(jnp.int32)[None]
    stations = delays.shape[1] * lax.axis_size("stn")
    amplitude = 1.0 / math.sqrt(stations // SUBARRAYS)
    partial = beam_sums(
        own, following, taps, delays, station_sub, beam_sub, chan_start, amplitude
    )
    summed = lax.psum_scatter(partial, "stn", scatter_dimension=0, tiled=True)
    swapped = lax.all_to_all(summed, "chan", split_axis=0, concat_axis=2, tiled=True)
    swapped = lax.all_to_all(swapped, "beam", split_axis=0, concat_axis=3, tiled=True)
    return swapped.astype(jnp.float32)


def solution(mesh):
    placed = (P(None, "stn", "chan", "beam"), P(), P(None, "stn"), P("stn"), P())
    return jax.shard_map(
        body,
        mesh=mesh,
        in_specs=placed,
        out_specs=P(("stn", "chan", "beam"), None, None, None, None),
        check_vma=False,
    )
```

```python
import functools
import math

import jax
import jax.numpy as jnp
import numpy as np
from jax import lax
from jax.experimental import pallas as pl
from jax.experimental.pallas import tpu as pltpu
from jax.sharding import PartitionSpec as P

SUBARRAYS = 4
UNROLL = 4
LANES = 128
MESH = pl.DeviceIdType.MESH


def dft_tables(fine):
    index = np.arange(fine)
    angle = 2.0 * np.pi * (index[:, None] * index[None, :] % fine) / fine
    scale = 1.0 / math.sqrt(fine)
    return (
        jnp.asarray(np.cos(angle) * scale, jnp.bfloat16),
        jnp.asarray(np.sin(angle) * scale, jnp.bfloat16),
    )


def unit_turn(turn):
    quarter = (turn + 8192) >> 14
    t = (turn - (quarter << 14)).astype(jnp.float32) * (2.0 * math.pi / 65536.0)
    u = t * t
    sine = t * (1.0 + u * (-1.0 / 6 + u * (1.0 / 120 + u * (-1.0 / 5040))))
    cosine = 1.0 + u * (-0.5 + u * (1.0 / 24 + u * (-1.0 / 720 + u * (1.0 / 40320))))
    odd = (quarter & 1) == 1
    c = jnp.where(odd, sine, cosine)
    s = jnp.where(odd, cosine, sine)
    c = jnp.where(((quarter + 1) & 2) == 2, -c, c)
    s = jnp.where((quarter & 2) == 2, -s, s)
    return c, s


def beam_kernel(
    amplitude,
    station_sub,
    beam_sub,
    start,
    turns_ref,
    taps_ref,
    cos_ref,
    sin_ref,
    own_ref,
    next_ref,
    out_ref,
    table,
    wide,
    half,
    filtered,
    spec,
    x_ref,
    w_ref,
    delay_ref,
    members,
    counts,
):
    tap_count, fine = taps_ref.shape
    stations = own_ref.shape[2]
    samples = own_ref.shape[3]
    beams, frames = out_ref.shape[2:4]
    groups = frames // 4
    parts = fine // LANES
    row = stations + UNROLL
    chan = pl.program_id(0)

    @pl.when(chan == 0)
    def _():
        for sub in range(SUBARRAYS):
            def add(s, n, sub=sub):
                members[sub * row + n] = s
                return n + jnp.where(station_sub[s] == sub, 1, 0)

            count = lax.fori_loop(0, stations, add, jnp.int32(0))
            for extra in range(UNROLL):
                members[sub * row + count + extra] = stations
            counts[sub] = (count + UNROLL - 1) // UNROLL
        for part in range(2 * parts):
            x_ref[part, stations] = jnp.zeros((frames, LANES), jnp.float32)
            w_ref[part, pl.ds(stations, 8), :] = jnp.zeros((8, LANES), jnp.float32)
        for b in range(beams):
            delay_ref[b] = jnp.broadcast_to(turns_ref[:, b : b + 1], (stations, LANES))
        cosine = cos_ref[...].astype(jnp.float32)
        sine = sin_ref[...].astype(jnp.float32)
        k = lax.broadcasted_iota(jnp.int32, (fine, fine), 1)
        for phase in range(4):
            q = (3 * phase * k) & 3
            cq = jnp.where(q == 0, 1.0, jnp.where(q == 2, -1.0, 0.0))
            sq = jnp.where(q == 1, 1.0, jnp.where(q == 3, -1.0, 0.0))
            same = (cosine * cq - sine * sq).astype(jnp.bfloat16)
            cross = sine * cq + cosine * sq
            table[phase, 0:fine, 0:fine] = same
            table[phase, fine:, fine:] = same
            table[phase, fine:, 0:fine] = cross.astype(jnp.bfloat16)
            table[phase, 0:fine, fine:] = (-cross).astype(jnp.bfloat16)

    for ri in range(2):
        wide[ri, :, 0:samples] = own_ref[ri, 0].astype(jnp.float32)
        wide[ri, :, samples:] = next_ref[ri, 0].astype(jnp.float32)
        shift = fine // 4
        length = half.shape[2]
        half[ri] = wide[ri, :, shift : shift + length]

    hop = 3 * fine // 4

    @pl.loop(0, groups)
    def _(g):
        for phase in range(4):
            source = wide if phase % 2 == 0 else half
            base = phase * hop - (0 if phase % 2 == 0 else fine // 4)
            for ri in range(2):
                total = None
                for tap in range(tap_count):
                    at = pl.multiple_of(g * 3 * fine + (base + tap * fine), LANES)
                    term = taps_ref[tap : tap + 1, :] * source[ri, :, pl.ds(at, fine)]
                    total = term if total is None else total + term
                filtered[phase, pl.ds(pl.multiple_of(g * stations, stations), stations), ri * fine : (ri + 1) * fine] = (
                    total.astype(jnp.bfloat16)
                )

    for phase in range(4):
        result = jnp.dot(filtered[phase], table[phase], preferred_element_type=jnp.float32)
        for g in range(groups):
            at = (4 * g + phase) * stations
            for part in range(2 * parts):
                spec[part, at : at + stations, :] = result[
                    g * stations : (g + 1) * stations, part * LANES : (part + 1) * LANES
                ]
    for s in range(stations):
        for part in range(2 * parts):
            x_ref[part, s] = spec.at[part][pl.ds(s, frames, stride=stations), :]

    lane = lax.broadcasted_iota(jnp.int32, (stations, LANES), 1)
    first = (start[0] + chan) * fine

    @pl.loop(0, beams)
    def _(b):
        delay = delay_ref[b]
        for part in range(parts):
            turn = (delay * (lane + (first + part * LANES))) & 65535
            c, s = unit_turn(turn)
            w_ref[part, 0:stations, :] = c * amplitude
            w_ref[parts + part, 0:stations, :] = s * (-amplitude)
        sub = beam_sub[b]

        def add(i, carry):
            totals = list(carry)
            for u in range(UNROLL):
                s = members[sub * row + i * UNROLL + u]
                for part in range(parts):
                    w_re = w_ref.at[part][pl.ds(s, 8, stride=0), :][None]
                    w_im = w_ref.at[parts + part][pl.ds(s, 8, stride=0), :][None]
                    x_re = x_ref[part, s].reshape(frames // 8, 8, LANES)
                    x_im = x_ref[parts + part, s].reshape(frames // 8, 8, LANES)
                    totals[part] = totals[part] + (w_re * x_re - w_im * x_im)
                    totals[parts + part] = totals[parts + part] + (w_re * x_im + w_im * x_re)
            return tuple(totals)

        zero = jnp.zeros((frames // 8, 8, LANES), jnp.float32)
        totals = lax.fori_loop(0, counts[sub], add, (zero,) * (2 * parts))
        for part in range(parts):
            lanes = slice(part * LANES, (part + 1) * LANES)
            out_ref[0, 0, b, :, lanes] = totals[part].reshape(frames, LANES).astype(jnp.bfloat16)
            out_ref[0, 1, b, :, lanes] = totals[parts + part].reshape(frames, LANES).astype(jnp.bfloat16)


def beam_sums(own, following, taps, delays, station_sub, beam_sub, chan_start, amplitude):
    tap_count, fine = taps.shape
    chans, stations, samples = own.shape[1:]
    beams = delays.shape[0]
    hop = 3 * fine // 4
    frames = samples // hop
    parts = fine // LANES
    cosine, sine = dft_tables(fine)
    whole = lambda *shape: pl.BlockSpec(shape, lambda c, *_: (0,) * len(shape))
    volts_spec = pl.BlockSpec((2, 1, stations, samples), lambda c, *_: (0, c, 0, 0))
    length = 2 * samples - LANES
    return pl.pallas_call(
        functools.partial(beam_kernel, amplitude),
        out_shape=jax.ShapeDtypeStruct((chans, 2, beams, frames, fine), jnp.bfloat16),
        grid_spec=pltpu.PrefetchScalarGridSpec(
            num_scalar_prefetch=3,
            grid=(chans,),
            in_specs=[
                whole(stations, beams),
                whole(tap_count, fine),
                whole(fine, fine),
                whole(fine, fine),
                volts_spec,
                volts_spec,
            ],
            out_specs=pl.BlockSpec((1, 2, beams, frames, fine), lambda c, *_: (c, 0, 0, 0, 0)),
            scratch_shapes=[
                pltpu.VMEM((4, 2 * fine, 2 * fine), jnp.bfloat16),
                pltpu.VMEM((2, stations, 2 * samples), jnp.float32),
                pltpu.VMEM((2, stations, length), jnp.float32),
                pltpu.VMEM((4, frames // 4 * stations, 2 * fine), jnp.bfloat16),
                pltpu.VMEM((2 * parts, (frames + 1) * stations, LANES), jnp.float32),
                pltpu.VMEM((2 * parts, stations + 1, frames, LANES), jnp.float32),
                pltpu.VMEM((2 * parts, stations + 8, LANES), jnp.float32),
                pltpu.VMEM((beams, stations, LANES), jnp.int32),
                pltpu.SMEM((SUBARRAYS * (stations + UNROLL),), jnp.int32),
                pltpu.SMEM((SUBARRAYS,), jnp.int32),
            ],
        ),
        compiler_params=pltpu.CompilerParams(dimension_semantics=("arbitrary",)),
        name="beam_sums",
    )(station_sub, beam_sub, chan_start, delays.T, taps, cosine, sine, own, following)


def exchange_kernel(sizes, part_ref, out_ref, *scratch):
    n_chan, n_core, bits = sizes
    received, sent = scratch[:bits], scratch[bits : 2 * bits - 1]
    total, send, recv, far_send, far_recv, own_sem = scratch[2 * bits - 1 :]
    chans = part_ref.shape[0]
    per_device = total.shape[3]
    stn, chan, core = (lax.axis_index(name) for name in ("stn", "chan", "beam"))
    own_bit = [(stn // 2 ** (bits - 1 - dim)) % 2 for dim in range(bits)]
    orders = (tuple(range(bits - 1, -1, -1)), tuple(range(bits)))

    def partner(dim):
        return (stn + (1 - 2 * own_bit[dim]) * 2 ** (bits - 1 - dim), chan, core)

    def far(dz, dc):
        return ((chan + dz) % n_chan, (core + dc) % n_core)

    offsets = [(dz, dc) for dz in range(n_chan) for dc in range(n_core)]
    barrier = pltpu.get_barrier_semaphore()
    peers = [partner(dim) for dim in range(bits)] + [(stn, *far(dz, dc)) for dz, dc in offsets[1:]]
    for peer in peers:
        pl.semaphore_signal(barrier, inc=1, device_id=peer, device_id_type=MESH)
    pl.semaphore_wait(barrier, len(peers))

    def region(ri, stage, last):
        order = orders[ri]
        index = [slice(None)] * bits
        for dim in order[:stage]:
            index[dim] = own_bit[dim]
        if stage < bits:
            index[order[stage]] = last(order[stage])
        return index

    def other(dim):
        return 1 - own_bit[dim]

    def with_received(c, ri, stage, index):
        value = part_ref[(c, ri, *index)].astype(jnp.float32)
        for earlier in range(stage):
            kept = [dim for dim in range(bits) if dim not in orders[ri][: earlier + 1]]
            piece = received[earlier][(c, ri, *(index[dim] for dim in kept))]
            value = value + piece.astype(jnp.float32)
        return value

    def hop(c, ri, stage):
        if stage == 0:
            source = part_ref.at[(c, ri, *region(ri, 0, other))]
        else:
            source = sent[stage - 1].at[c, ri]
        return pltpu.make_async_remote_copy(
            src_ref=source,
            dst_ref=received[stage].at[c, ri],
            send_sem=send.at[stage, c, ri],
            recv_sem=recv.at[stage, c, ri],
            device_id=partner(orders[ri][stage]),
            device_id_type=MESH,
        )

    def deliver(c, number):
        z, k = far(*offsets[number])
        return pltpu.make_async_remote_copy(
            src_ref=total.at[c, z, k],
            dst_ref=out_ref.at[:, :, chan * chans + c, core],
            send_sem=far_send.at[c, number],
            recv_sem=far_recv.at[c, number],
            device_id=(stn, z, k),
            device_id_type=MESH,
        )

    def keep(c):
        return pltpu.make_async_copy(
            total.at[c, chan, core], out_ref.at[:, :, chan * chans + c, core], own_sem.at[c]
        )

    def step(c, stage):
        if stage == 0:
            for ri in range(2):
                hop(c, ri, 0).start()
            return
        for ri in range(2):
            hop(c, ri, stage - 1).wait_recv()
            if stage < bits:
                sent[stage - 1][c, ri] = with_received(
                    c, ri, stage, region(ri, stage, other)
                ).astype(jnp.bfloat16)
            else:
                value = with_received(c, ri, stage, own_bit).astype(jnp.bfloat16)
                value = value.reshape((n_chan, n_core, per_device) + value.shape[1:])
                total[c, :, :, :, ri] = value
        if stage < bits:
            for ri in range(2):
                hop(c, ri, stage).start()
        else:
            for number in range(len(offsets) - 1, 0, -1):
                deliver(c, number).start()
            keep(c).start()

    for tick in range(chans + bits):
        for c in reversed(range(chans)):
            if 0 <= tick - c <= bits:
                step(c, tick - c)

    for c in range(chans):
        for ri in range(2):
            for stage in range(bits):
                hop(c, ri, stage).wait_send()
        for number in range(1, len(offsets)):
            deliver(c, number).wait()
        keep(c).wait()


def exchange(partial):
    chans, _, beams, frames, fine = partial.shape
    n_stn, n_chan, n_core = (lax.axis_size(name) for name in ("stn", "chan", "beam"))
    bits = n_stn.bit_length() - 1
    assert n_stn == 2**bits
    per = beams // n_stn
    per_device = per // (n_chan * n_core)
    peers = n_chan * n_core
    block = (per, frames, fine)
    halves = [pltpu.VMEM((chans, 2) + (2,) * (bits - 1 - t) + block, jnp.bfloat16) for t in range(bits)]
    out = pl.pallas_call(
        functools.partial(exchange_kernel, (n_chan, n_core, bits)),
        out_shape=jax.ShapeDtypeStruct(
            (per_device, 2, n_chan * chans, n_core, frames, fine), jnp.bfloat16
        ),
        in_specs=[pl.BlockSpec(memory_space=pltpu.VMEM)],
        out_specs=pl.BlockSpec(memory_space=pl.ANY),
        scratch_shapes=[
            *halves,
            *halves[1:],
            pltpu.VMEM((chans, n_chan, n_core, per_device, 2, frames, fine), jnp.bfloat16),
            pltpu.SemaphoreType.DMA((bits, chans, 2)),
            pltpu.SemaphoreType.DMA((bits, chans, 2)),
            pltpu.SemaphoreType.DMA((chans, peers)),
            pltpu.SemaphoreType.DMA((chans, peers)),
            pltpu.SemaphoreType.DMA((chans,)),
        ],
        compiler_params=pltpu.CompilerParams(collective_id=0, has_side_effects=True),
        name="exchange",
    )(partial.reshape((chans, 2) + (2,) * bits + block))
    return out.reshape(per_device, 2, n_chan * chans, n_core * frames, fine)


def body(volts, taps, delays, station_sub, beam_sub):
    own = jnp.transpose(volts, (0, 2, 1, 3))
    size = lax.axis_size("beam")
    following = lax.ppermute(own, "beam", [(i, i - 1) for i in range(1, size)])
    chans = own.shape[1]
    chan_start = (lax.axis_index("chan") * chans).astype(jnp.int32)[None]
    stations = delays.shape[1] * lax.axis_size("stn")
    amplitude = 1.0 / math.sqrt(stations // SUBARRAYS)
    partial = beam_sums(
        own, following, taps, delays, station_sub, beam_sub, chan_start, amplitude
    )
    return exchange(partial).astype(jnp.float32)


def solution(mesh):
    placed = (P(None, "stn", "chan", "beam"), P(), P(None, "stn"), P("stn"), P())
    return jax.shard_map(
        body,
        mesh=mesh,
        in_specs=placed,
        out_specs=P(("stn", "chan", "beam"), None, None, None, None),
        check_vma=False,
    )
```

```python
import functools
import math

import jax
import jax.numpy as jnp
import numpy as np
from jax import lax
from jax.experimental import pallas as pl
from jax.experimental.pallas import tpu as pltpu
from jax.sharding import PartitionSpec as P

SUBARRAYS = 4
UNROLL = 4
LANES = 128
VMEM_LIMIT = 32 * 2**20
MESH = pl.DeviceIdType.MESH


def dft_tables(fine):
    index = np.arange(fine)
    angle = 2.0 * np.pi * (index[:, None] * index[None, :] % fine) / fine
    scale = 1.0 / math.sqrt(fine)
    return (
        jnp.asarray(np.cos(angle) * scale, jnp.bfloat16),
        jnp.asarray(np.sin(angle) * scale, jnp.bfloat16),
    )


def unit_turn(turn):
    quarter = (turn + 8192) >> 14
    t = (turn - (quarter << 14)).astype(jnp.float32) * (2.0 * math.pi / 65536.0)
    u = t * t
    sine = t * (1.0 + u * (-1.0 / 6 + u * (1.0 / 120 + u * (-1.0 / 5040))))
    cosine = 1.0 + u * (-0.5 + u * (1.0 / 24 + u * (-1.0 / 720 + u * (1.0 / 40320))))
    odd = (quarter & 1) == 1
    c = jnp.where(odd, sine, cosine)
    s = jnp.where(odd, cosine, sine)
    c = jnp.where(((quarter + 1) & 2) == 2, -c, c)
    s = jnp.where((quarter & 2) == 2, -s, s)
    return c, s


def beam_kernel(
    amplitude,
    station_sub,
    beam_sub,
    start,
    turns_ref,
    taps_ref,
    cos_ref,
    sin_ref,
    own_ref,
    next_ref,
    out_ref,
    table,
    wide,
    half,
    filtered,
    spec,
    x_ref,
    w_ref,
    delay_ref,
    members,
    counts,
):
    tap_count, fine = taps_ref.shape
    stations = own_ref.shape[2]
    samples = own_ref.shape[3]
    beams, frames = out_ref.shape[2:4]
    groups = frames // 4
    parts = fine // LANES
    row = stations + UNROLL
    chan = pl.program_id(0)

    @pl.when(chan == 0)
    def _():
        for sub in range(SUBARRAYS):
            def add(s, n, sub=sub):
                members[sub * row + n] = s
                return n + jnp.where(station_sub[s] == sub, 1, 0)

            count = lax.fori_loop(0, stations, add, jnp.int32(0))
            for extra in range(UNROLL):
                members[sub * row + count + extra] = stations
            counts[sub] = (count + UNROLL - 1) // UNROLL
        for part in range(2 * parts):
            x_ref[part, stations] = jnp.zeros((frames, LANES), jnp.float32)
            w_ref[part, pl.ds(stations, 8), :] = jnp.zeros((8, LANES), jnp.float32)
        for b in range(beams):
            delay_ref[b] = jnp.broadcast_to(turns_ref[:, b : b + 1], (stations, LANES))
        cosine = cos_ref[...].astype(jnp.float32)
        sine = sin_ref[...].astype(jnp.float32)
        k = lax.broadcasted_iota(jnp.int32, (fine, fine), 1)
        for phase in range(4):
            q = (3 * phase * k) & 3
            cq = jnp.where(q == 0, 1.0, jnp.where(q == 2, -1.0, 0.0))
            sq = jnp.where(q == 1, 1.0, jnp.where(q == 3, -1.0, 0.0))
            same = (cosine * cq - sine * sq).astype(jnp.bfloat16)
            cross = sine * cq + cosine * sq
            table[phase, 0:fine, 0:fine] = same
            table[phase, fine:, fine:] = same
            table[phase, fine:, 0:fine] = cross.astype(jnp.bfloat16)
            table[phase, 0:fine, fine:] = (-cross).astype(jnp.bfloat16)

    for ri in range(2):
        wide[ri, :, 0:samples] = own_ref[ri, 0].astype(jnp.float32)
        wide[ri, :, samples:] = next_ref[ri, 0].astype(jnp.float32)
        shift = fine // 4
        length = half.shape[2]
        half[ri] = wide[ri, :, shift : shift + length]

    hop = 3 * fine // 4

    @pl.loop(0, groups)
    def _(g):
        for phase in range(4):
            source = wide if phase % 2 == 0 else half
            base = phase * hop - (0 if phase % 2 == 0 else fine // 4)
            for ri in range(2):
                total = None
                for tap in range(tap_count):
                    at = pl.multiple_of(g * 3 * fine + (base + tap * fine), LANES)
                    term = taps_ref[tap : tap + 1, :] * source[ri, :, pl.ds(at, fine)]
                    total = term if total is None else total + term
                filtered[phase, pl.ds(pl.multiple_of(g * stations, stations), stations), ri * fine : (ri + 1) * fine] = (
                    total.astype(jnp.bfloat16)
                )

    for phase in range(4):
        result = jnp.dot(filtered[phase], table[phase], preferred_element_type=jnp.float32)
        for g in range(groups):
            at = (4 * g + phase) * stations
            for part in range(2 * parts):
                spec[part, at : at + stations, :] = result[
                    g * stations : (g + 1) * stations, part * LANES : (part + 1) * LANES
                ]
    for s in range(stations):
        for part in range(2 * parts):
            x_ref[part, s] = spec.at[part][pl.ds(s, frames, stride=stations), :]

    lane = lax.broadcasted_iota(jnp.int32, (stations, LANES), 1)
    first = (start[0] + chan) * fine

    @pl.loop(0, beams)
    def _(b):
        delay = delay_ref[b]
        for part in range(parts):
            turn = (delay * (lane + (first + part * LANES))) & 65535
            c, s = unit_turn(turn)
            w_ref[part, 0:stations, :] = c * amplitude
            w_ref[parts + part, 0:stations, :] = s * (-amplitude)
        sub = beam_sub[b]

        def add(i, carry):
            totals = list(carry)
            for u in range(UNROLL):
                s = members[sub * row + i * UNROLL + u]
                for part in range(parts):
                    w_re = w_ref.at[part][pl.ds(s, 8, stride=0), :][None]
                    w_im = w_ref.at[parts + part][pl.ds(s, 8, stride=0), :][None]
                    x_re = x_ref[part, s].reshape(frames // 8, 8, LANES)
                    x_im = x_ref[parts + part, s].reshape(frames // 8, 8, LANES)
                    totals[part] = totals[part] + (w_re * x_re - w_im * x_im)
                    totals[parts + part] = totals[parts + part] + (w_re * x_im + w_im * x_re)
            return tuple(totals)

        zero = jnp.zeros((frames // 8, 8, LANES), jnp.float32)
        totals = lax.fori_loop(0, counts[sub], add, (zero,) * (2 * parts))
        for part in range(parts):
            lanes = slice(part * LANES, (part + 1) * LANES)
            out_ref[0, 0, b, :, lanes] = totals[part].reshape(frames, LANES).astype(jnp.bfloat16)
            out_ref[0, 1, b, :, lanes] = totals[parts + part].reshape(frames, LANES).astype(jnp.bfloat16)


def beam_sums(own, following, taps, delays, station_sub, beam_sub, chan_start, amplitude):
    tap_count, fine = taps.shape
    chans, stations, samples = own.shape[1:]
    beams = delays.shape[0]
    hop = 3 * fine // 4
    frames = samples // hop
    parts = fine // LANES
    cosine, sine = dft_tables(fine)
    whole = lambda *shape: pl.BlockSpec(shape, lambda c, *_: (0,) * len(shape))
    volts_spec = pl.BlockSpec((2, 1, stations, samples), lambda c, *_: (0, c, 0, 0))
    length = 2 * samples - LANES
    return pl.pallas_call(
        functools.partial(beam_kernel, amplitude),
        out_shape=jax.ShapeDtypeStruct((chans, 2, beams, frames, fine), jnp.bfloat16),
        grid_spec=pltpu.PrefetchScalarGridSpec(
            num_scalar_prefetch=3,
            grid=(chans,),
            in_specs=[
                whole(stations, beams),
                whole(tap_count, fine),
                whole(fine, fine),
                whole(fine, fine),
                volts_spec,
                volts_spec,
            ],
            out_specs=pl.BlockSpec((1, 2, beams, frames, fine), lambda c, *_: (c, 0, 0, 0, 0)),
            scratch_shapes=[
                pltpu.VMEM((4, 2 * fine, 2 * fine), jnp.bfloat16),
                pltpu.VMEM((2, stations, 2 * samples), jnp.float32),
                pltpu.VMEM((2, stations, length), jnp.float32),
                pltpu.VMEM((4, frames // 4 * stations, 2 * fine), jnp.bfloat16),
                pltpu.VMEM((2 * parts, (frames + 1) * stations, LANES), jnp.float32),
                pltpu.VMEM((2 * parts, stations + 1, frames, LANES), jnp.float32),
                pltpu.VMEM((2 * parts, stations + 8, LANES), jnp.float32),
                pltpu.VMEM((beams, stations, LANES), jnp.int32),
                pltpu.SMEM((SUBARRAYS * (stations + UNROLL),), jnp.int32),
                pltpu.SMEM((SUBARRAYS,), jnp.int32),
            ],
        ),
        compiler_params=pltpu.CompilerParams(
            dimension_semantics=("arbitrary",), vmem_limit_bytes=VMEM_LIMIT
        ),
        name="beam_sums",
    )(station_sub, beam_sub, chan_start, delays.T, taps, cosine, sine, own, following)


def exchange_kernel(sizes, part_ref, out_ref, *scratch):
    n_chan, n_core, bits = sizes
    received, sent = scratch[:bits], scratch[bits : 2 * bits - 1]
    total, send, recv, far_send, far_recv, own_sem = scratch[2 * bits - 1 :]
    chans = part_ref.shape[0]
    per_device = total.shape[3]
    stn, chan, core = (lax.axis_index(name) for name in ("stn", "chan", "beam"))
    own_bit = [(stn // 2 ** (bits - 1 - dim)) % 2 for dim in range(bits)]
    orders = (tuple(range(bits - 1, -1, -1)), tuple(range(bits)))

    def partner(dim):
        return (stn + (1 - 2 * own_bit[dim]) * 2 ** (bits - 1 - dim), chan, core)

    def far(dz, dc):
        return ((chan + dz) % n_chan, (core + dc) % n_core)

    offsets = [(dz, dc) for dz in range(n_chan) for dc in range(n_core)]
    barrier = pltpu.get_barrier_semaphore()
    peers = [partner(dim) for dim in range(bits)] + [(stn, *far(dz, dc)) for dz, dc in offsets[1:]]
    for peer in peers:
        pl.semaphore_signal(barrier, inc=1, device_id=peer, device_id_type=MESH)
    pl.semaphore_wait(barrier, len(peers))

    def region(ri, stage, last):
        order = orders[ri]
        index = [slice(None)] * bits
        for dim in order[:stage]:
            index[dim] = own_bit[dim]
        if stage < bits:
            index[order[stage]] = last(order[stage])
        return index

    def other(dim):
        return 1 - own_bit[dim]

    def with_received(c, ri, stage, index):
        value = part_ref[(c, ri, *index)].astype(jnp.float32)
        for earlier in range(stage):
            kept = [dim for dim in range(bits) if dim not in orders[ri][: earlier + 1]]
            piece = received[earlier][(c, ri, *(index[dim] for dim in kept))]
            value = value + piece.astype(jnp.float32)
        return value

    def hop(c, ri, stage):
        if stage == 0:
            source = part_ref.at[(c, ri, *region(ri, 0, other))]
        else:
            source = sent[stage - 1].at[c, ri]
        return pltpu.make_async_remote_copy(
            src_ref=source,
            dst_ref=received[stage].at[c, ri],
            send_sem=send.at[stage, c, ri],
            recv_sem=recv.at[stage, c, ri],
            device_id=partner(orders[ri][stage]),
            device_id_type=MESH,
        )

    def deliver(c, number):
        z, k = far(*offsets[number])
        return pltpu.make_async_remote_copy(
            src_ref=total.at[c, z, k],
            dst_ref=out_ref.at[:, :, chan * chans + c, core],
            send_sem=far_send.at[c, number],
            recv_sem=far_recv.at[c, number],
            device_id=(stn, z, k),
            device_id_type=MESH,
        )

    def keep(c):
        return pltpu.make_async_copy(
            total.at[c, chan, core], out_ref.at[:, :, chan * chans + c, core], own_sem.at[c]
        )

    def step(c, stage):
        if stage == 0:
            for ri in range(2):
                hop(c, ri, 0).start()
            return
        for ri in range(2):
            hop(c, ri, stage - 1).wait_recv()
            if stage < bits:
                sent[stage - 1][c, ri] = with_received(
                    c, ri, stage, region(ri, stage, other)
                ).astype(jnp.bfloat16)
            else:
                value = with_received(c, ri, stage, own_bit).astype(jnp.bfloat16)
                value = value.reshape((n_chan, n_core, per_device) + value.shape[1:])
                total[c, :, :, :, ri] = value
        if stage < bits:
            for ri in range(2):
                hop(c, ri, stage).start()
        else:
            for number in range(len(offsets) - 1, 0, -1):
                deliver(c, number).start()
            keep(c).start()

    for tick in range(chans + bits):
        for c in reversed(range(chans)):
            if 0 <= tick - c <= bits:
                step(c, tick - c)

    for c in range(chans):
        for ri in range(2):
            for stage in range(bits):
                hop(c, ri, stage).wait_send()
        for number in range(1, len(offsets)):
            deliver(c, number).wait()
        keep(c).wait()


def exchange(partial):
    chans, _, beams, frames, fine = partial.shape
    n_stn, n_chan, n_core = (lax.axis_size(name) for name in ("stn", "chan", "beam"))
    bits = n_stn.bit_length() - 1
    assert n_stn == 2**bits
    per = beams // n_stn
    per_device = per // (n_chan * n_core)
    peers = n_chan * n_core
    block = (per, frames, fine)
    halves = [pltpu.VMEM((chans, 2) + (2,) * (bits - 1 - t) + block, jnp.bfloat16) for t in range(bits)]
    out = pl.pallas_call(
        functools.partial(exchange_kernel, (n_chan, n_core, bits)),
        out_shape=jax.ShapeDtypeStruct(
            (per_device, 2, n_chan * chans, n_core, frames, fine), jnp.bfloat16
        ),
        in_specs=[pl.BlockSpec(memory_space=pltpu.VMEM)],
        out_specs=pl.BlockSpec(memory_space=pl.ANY),
        scratch_shapes=[
            *halves,
            *halves[1:],
            pltpu.VMEM((chans, n_chan, n_core, per_device, 2, frames, fine), jnp.bfloat16),
            pltpu.SemaphoreType.DMA((bits, chans, 2)),
            pltpu.SemaphoreType.DMA((bits, chans, 2)),
            pltpu.SemaphoreType.DMA((chans, peers)),
            pltpu.SemaphoreType.DMA((chans, peers)),
            pltpu.SemaphoreType.DMA((chans,)),
        ],
        compiler_params=pltpu.CompilerParams(
            collective_id=0, has_side_effects=True, vmem_limit_bytes=VMEM_LIMIT
        ),
        name="exchange",
    )(partial.reshape((chans, 2) + (2,) * bits + block))
    return out.reshape(per_device, 2, n_chan * chans, n_core * frames, fine)


def body(volts, taps, delays, station_sub, beam_sub):
    own = jnp.transpose(volts, (0, 2, 1, 3))
    size = lax.axis_size("beam")
    following = lax.ppermute(own, "beam", [(i, i - 1) for i in range(1, size)])
    chans = own.shape[1]
    chan_start = (lax.axis_index("chan") * chans).astype(jnp.int32)[None]
    stations = delays.shape[1] * lax.axis_size("stn")
    amplitude = 1.0 / math.sqrt(stations // SUBARRAYS)
    partial = beam_sums(
        own, following, taps, delays, station_sub, beam_sub, chan_start, amplitude
    )
    return exchange(partial).astype(jnp.float32)


def solution(mesh):
    placed = (P(None, "stn", "chan", "beam"), P(), P(None, "stn"), P("stn"), P())
    return jax.shard_map(
        body,
        mesh=mesh,
        in_specs=placed,
        out_specs=P(("stn", "chan", "beam"), None, None, None, None),
        check_vma=False,
    )
```
